32 devices in a mesh: wide: 16 (over z, y, core), narrow: 2 (over x).
Axes of the slice: x: 2, y: 2, z: 4, core: 2. Of those that a mesh axis runs over, the one named last changes fastest.
Arguments:
- concentrations: float32 [256, 32, 256], P('wide', 'narrow'), may hold values from 0.1 to 2
- wind_speeds: bfloat16 [2, 2, 32, 256], P(None, None, ('narrow', 'wide')), may hold values from -0.59765625 to 0.59765625
- rate_constants: float32 [768], replicated, may hold values from 0.05 to 1
- reactants: int32 [768, 2], replicated, may hold values from 0 to 255
- products: int32 [768, 2], replicated, may hold values from 0 to 255
Outputs:
- after_chemistry: float32 [256, 32, 256], P(None, ('narrow', 'wide'))
The draws below stay inside these ranges and needn't reach their ends.
Inputs may be any that keep to these rules, and one draw needn't show every extreme that they name: `reactants`: each entry is a species number. `products`: each entry is a species number.
All inputs are finite; a program needn't handle non-finite values.
Results may differ from the reference program's by a relative error of at most 0.0003.
Values may be sent and summed in bfloat16 or wider, within the bound.
A program may use at most 64 MiB of HBM per device.

```python
import math
import jax
import jax.numpy as jnp
from jax import lax

S = 256
R = 768
NY = 256
SUB = 2
SECTIONS = 6
NX = 32
N_NARROW = 2


def place_ends(result, key, low, high):
    longest = result.shape.index(max(result.shape))
    spots = []
    for shift in (0, 1):
        where = [jax.random.randint(jax.random.fold_in(key, axis), (), 0, length) for axis, length in enumerate(result.shape)]
        where[longest] = (where[longest] + shift) % result.shape[longest]
        spots.append(tuple(where))
    return result.at[spots[0]].set(low).at[spots[1]].set(high)


def block_scale(own_key, extent, shards, smallest, high):
    def one(dim, blocks):
        steps = jax.random.uniform(jax.random.fold_in(jax.random.fold_in(own_key, 6), dim), (blocks,), jnp.float32, smallest / len(shards), high / len(shards))
        return jnp.repeat(jnp.exp(steps), extent[dim] // blocks).reshape((-1,) + (1,) * (len(extent) - dim - 1))

    gain = one(*shards[0])
    for cut in shards[1:]:
        gain = gain * one(*cut)
    return gain


def setup_inputs(seed: int = 0) -> dict:
    keys = jax.random.split(jax.random.key(seed), 6)
    return {
        "concentrations": jnp.clip(jnp.exp(math.log(2.0) - 2.9957323 * jax.random.uniform(keys[0], (S, NX, NY), jnp.float32) ** block_scale(keys[0], (S, NX, NY), ((0, 16), (1, 2)), -0.2, 0.2)), 0.1, 2.0),
        "wind_speeds": jnp.clip(jax.random.uniform(keys[1], (SUB, 2, NX, NY), jnp.float32, -0.59765625, 0.59765625) * block_scale(keys[1], (SUB, 2, NX, NY), ((2, 32),), -0.4, 0.0), -0.59765625, 0.59765625).astype(jnp.bfloat16),
        "rate_constants": jnp.clip(jnp.exp(jax.random.uniform(keys[2], (R,), jnp.float32, math.log(0.05), math.log(1.0))), 0.05, 1.0),
        "reactants": place_ends(jax.random.randint(keys[3], (R, 2), 0, S), jax.random.fold_in(keys[3], 1), 0, S - 1).astype(jnp.int32),
        "products": place_ends(jax.random.randint(keys[4], (R, 2), 0, S), jax.random.fold_in(keys[4], 1), 0, S - 1).astype(jnp.int32),
    }


DIFFUSION = 0.1
CHEM_STEP = 0.02


def take_range(array, begin_at, end_at, along):
    along = along % array.ndim
    index = [slice(None)] * array.ndim
    index[along] = slice(begin_at, end_at)
    return array[tuple(index)]


def minmod(first_jump, second_jump):
    return jnp.maximum(0.0, jnp.minimum(first_jump, second_jump)) + jnp.minimum(0.0, jnp.maximum(first_jump, second_jump))


def sweep_axis(extended, speeds, along, closed):
    length = extended.shape[along]
    speed_face = 0.5 * (take_range(speeds, 0, length - 1, along) + take_range(speeds, 1, length, along))
    jumps = take_range(extended, 1, length, along) - take_range(extended, 0, length - 1, along)
    slopes = minmod(take_range(jumps, 0, length - 2, along), take_range(jumps, 1, length - 1, along))
    inner_speed = take_range(speed_face, 1, length - 2, along)
    left_value = take_range(extended, 1, length - 2, along) + 0.5 * (1.0 - inner_speed) * take_range(slopes, 0, length - 3, along)
    right_value = take_range(extended, 2, length - 1, along) - 0.5 * (1.0 + inner_speed) * take_range(slopes, 1, length - 2, along)
    face_flux = inner_speed * jnp.where(inner_speed >= 0.0, left_value, right_value) - DIFFUSION * take_range(jumps, 1, length - 2, along)
    if closed:
        position = lax.broadcasted_iota(jnp.int32, face_flux.shape, along % face_flux.ndim)
        face_flux = jnp.where((position > 0) & (position < length - 4), face_flux, 0.0)
    return take_range(extended, 2, length - 2, along) - (take_range(face_flux, 1, length - 3, along) - take_range(face_flux, 0, length - 4, along))


def sweep_second(tracer, speeds):
    pad_tracer = [(0, 0)] * (tracer.ndim - 1) + [(2, 2)]
    pad_speeds = [(0, 0)] * (speeds.ndim - 1) + [(2, 2)]
    return sweep_axis(jnp.pad(tracer, pad_tracer, mode="edge"), jnp.pad(speeds, pad_speeds, mode="edge"), -1, True)


def periodic(array):
    return jnp.concatenate([array[..., -2:, :], array, array[..., :2, :]], axis=-2)


def reference(concentrations, wind_speeds, rate_constants, reactants, products):
    tracer = concentrations
    speeds = wind_speeds.astype(jnp.float32)
    for substep in range(SUB):
        tracer = sweep_axis(periodic(tracer), periodic(speeds[substep, 0]), -2, False)
        tracer = sweep_second(tracer, speeds[substep, 1])
    blocks = tracer.reshape(S, N_NARROW, (NX // N_NARROW) * NY).transpose(1, 0, 2)

    def react_block(cell_block):
        for section_index in range(SECTIONS):
            rate_values = rate_constants[:, None] * cell_block[reactants[:, 0]] * cell_block[reactants[:, 1]]
            tendency = jax.ops.segment_sum(rate_values, products[:, 0], num_segments=S)
            tendency = tendency + jax.ops.segment_sum(rate_values, products[:, 1], num_segments=S)
            tendency = tendency - jax.ops.segment_sum(rate_values, reactants[:, 0], num_segments=S)
            tendency = tendency - jax.ops.segment_sum(rate_values, reactants[:, 1], num_segments=S)
            cell_block = cell_block + CHEM_STEP * tendency
        return cell_block

    reacted = lax.map(react_block, blocks)
    return reacted.transpose(1, 0, 2).reshape(S, NX, NY)
```

```python
import functools
import jax
import jax.numpy as jnp
from jax import lax
from jax.experimental import pallas as pl
from jax.experimental.pallas import tpu as pltpu
from jax.sharding import PartitionSpec as P

SECTIONS = 6
DIFFUSION = 0.1
CHEM_STEP = 0.02
HALO = 4
CHUNK = 4
MESH = pl.DeviceIdType.MESH
F32 = jnp.float32
BF16 = jnp.bfloat16


def minmod(first, second):
    return jnp.maximum(0.0, jnp.minimum(first, second)) + jnp.minimum(
        0.0, jnp.maximum(first, second)
    )


def coefficients(a):
    size = jnp.abs(a)
    return jnp.minimum(a, 0.0) - DIFFUSION, 0.5 * size * (1.0 - size), a >= 0.0


def sweep_rows(ext, wind):
    m = ext.shape[0] - 4
    a = 0.5 * (wind[1 : m + 2] + wind[2 : m + 3])
    jump_gain, slope_gain, forward = coefficients(a)
    jumps = ext[1:] - ext[:-1]
    slopes = minmod(jumps[:-1], jumps[1:])
    flux = (
        a * ext[1 : m + 2]
        + jump_gain * jumps[1 : m + 2]
        + slope_gain * jnp.where(forward, slopes[: m + 1], slopes[1:])
    )
    return ext[2 : m + 2] - (flux[1:] - flux[:-1])


def sweep_columns(q, wind):
    columns = q.shape[2]
    last = lax.broadcasted_iota(jnp.int32, wind.shape, 2) == columns - 1
    a = jnp.where(last, 0.0, 0.5 * (wind + pltpu.roll(wind, columns - 1, 2)))
    jump_gain, slope_gain, forward = coefficients(a)
    edge = lax.broadcasted_iota(jnp.int32, q.shape, 2) == columns - 1
    jumps = jnp.where(edge, 0.0, pltpu.roll(q, columns - 1, 2) - q)
    slopes = minmod(pltpu.roll(jumps, 1, 2), jumps)
    upwind = jnp.where(forward, slopes, pltpu.roll(slopes, columns - 1, 2))
    flux = a * q + jump_gain * jumps + slope_gain * upwind
    return q - (flux - pltpu.roll(flux, 1, 2))


def kernel(
    conc_ref, wind_ref, k_ref, react_ref, prod_ref, out_ref,
    ext, mid, done, winds, windf, incoming, cells, split, picks, net, gain, rates,
    wind_send, wind_recv, rim_send, rim_recv, halo_send, halo_recv, row_send, row_recv,
):
    wide = lax.axis_size("wide")
    narrow = lax.axis_size("narrow")
    me = lax.axis_index("wide")
    slab = lax.axis_index("narrow")
    groups, rows, columns = conc_ref.shape
    species = cells.shape[0]
    reactions = k_ref.shape[1]
    above = lax.rem(slab + 1, narrow)
    below = lax.rem(slab + narrow - 1, narrow)

    barrier = pltpu.get_barrier_semaphore()
    for step in range(1, wide):
        pl.semaphore_signal(
            barrier, inc=1, device_id={"wide": lax.rem(me + step, wide)}, device_id_type=MESH
        )
    for other in (above, below):
        pl.semaphore_signal(barrier, inc=1, device_id={"narrow": other}, device_id_type=MESH)

    ext[HALO : HALO + rows] = jnp.swapaxes(conc_ref[...], 0, 1)
    winds[HALO + me] = wind_ref[...]

    pl.semaphore_wait(barrier, wide + 1)

    def wind_copy(step):
        there = lax.rem(me + step, wide)
        return pltpu.make_async_remote_copy(
            src_ref=wind_ref,
            dst_ref=winds.at[HALO + me],
            send_sem=wind_send.at[step],
            recv_sem=wind_recv.at[me],
            device_id={"wide": there},
            device_id_type=MESH,
        )

    def halo_copies(buffer, send, recv):
        up = pltpu.make_async_remote_copy(
            src_ref=buffer.at[pl.ds(rows, HALO)],
            dst_ref=buffer.at[pl.ds(0, HALO)],
            send_sem=send.at[0],
            recv_sem=recv.at[0],
            device_id={"narrow": above},
            device_id_type=MESH,
        )
        down = pltpu.make_async_remote_copy(
            src_ref=buffer.at[pl.ds(HALO, HALO)],
            dst_ref=buffer.at[pl.ds(HALO + rows, HALO)],
            send_sem=send.at[1],
            recv_sem=recv.at[1],
            device_id={"narrow": below},
            device_id_type=MESH,
        )
        return up, down

    wind_copies = [wind_copy(step) for step in range(1, wide)]
    for copy in wind_copies:
        copy.start()
    halos = halo_copies(ext, halo_send, halo_recv)
    for copy in halos:
        copy.start()

    ids = lax.broadcasted_iota(jnp.int32, (species, reactions), 0)

    def one_hot(ref, which):
        return jnp.where(ids == ref[which : which + 1, :], 1.0, 0.0)

    first, second = one_hot(react_ref, 0), one_hot(react_ref, 1)
    net[...] = (one_hot(prod_ref, 0) + one_hot(prod_ref, 1) - first - second).astype(BF16)
    for index, table in enumerate((first, second)):
        turned = jnp.transpose(table).astype(BF16)
        picks[index, :, :species] = turned
        picks[index, :, species:] = turned
    gain[...] = jnp.transpose(jnp.broadcast_to(CHEM_STEP * k_ref[...], (columns, reactions)))

    for step in range(1, wide):
        source = lax.rem(me + wide - step, wide)
        pltpu.make_async_remote_copy(
            src_ref=wind_ref,
            dst_ref=winds.at[HALO + source],
            send_sem=wind_send.at[step],
            recv_sem=wind_recv.at[source],
            device_id={"wide": source},
            device_id_type=MESH,
        ).wait_recv()
    rims = halo_copies(winds, rim_send, rim_recv)
    for copy in rims:
        copy.start()
    windf[HALO : HALO + rows] = winds[HALO : HALO + rows].astype(F32)

    def wind_of(substep, direction, start, count):
        return windf[start : start + count, substep, direction : direction + 1, :]

    def first_substep(o):
        swept = sweep_rows(ext[o : o + CHUNK + 4], wind_of(0, 0, o, CHUNK + 4))
        mid[o : o + CHUNK] = sweep_columns(swept, wind_of(0, 1, o + 2, CHUNK))

    def second_substep(g):
        swept = sweep_rows(mid[g : g + CHUNK + 4], wind_of(1, 0, g + 2, CHUNK + 4))
        done[g : g + CHUNK] = sweep_columns(swept, wind_of(1, 1, g + 4, CHUNK))

    def row_copy(row):
        return pltpu.make_async_remote_copy(
            src_ref=done.at[row],
            dst_ref=incoming.at[me],
            send_sem=row_send.at[row],
            recv_sem=row_recv.at[me],
            device_id={"wide": row},
            device_id_type=MESH,
        )

    def send_row(row):
        @pl.when(row != me)
        def _():
            row_copy(row).start()

    inner = rows - 2 * HALO
    for o in range(HALO, rows, CHUNK):
        first_substep(o)
    for g in range(HALO, rows - HALO, CHUNK):
        second_substep(g)
    for k in range(inner):
        send_row(HALO + lax.rem(me + k, inner))

    for copy in halos + rims:
        copy.wait_recv()
    windf[0:HALO] = winds[0:HALO].astype(F32)
    windf[HALO + rows :] = winds[HALO + rows :].astype(F32)
    for o in (0, rows):
        first_substep(o)
    for g in (0, rows - HALO):
        second_substep(g)
    for k in range(2 * HALO):
        index = lax.rem(me + k, 2 * HALO)
        send_row(index + inner * (index // HALO))

    incoming[me] = done[me]
    for source in range(wide):
        @pl.when(source != me)
        def _():
            pltpu.make_async_remote_copy(
                src_ref=done.at[source],
                dst_ref=incoming.at[source],
                send_sem=row_send.at[source],
                recv_sem=row_recv.at[source],
                device_id={"wide": source},
                device_id_type=MESH,
            ).wait_recv()

    for source in range(wide):
        cells[source * groups : (source + 1) * groups] = incoming[source]

    block = species

    def section(_, carry):
        q = cells[...]
        high = q.astype(BF16)
        split[:species] = high
        split[species:] = (q - high.astype(F32)).astype(BF16)
        for start in range(0, reactions, block):
            span = pl.ds(start, block)
            one = jnp.dot(picks[0, span, :], split[...], preferred_element_type=F32)
            two = jnp.dot(picks[1, span, :], split[...], preferred_element_type=F32)
            rates[span, :] = (gain[span, :] * one * two).astype(BF16)
        cells[...] = q + jnp.dot(net[...], rates[...], preferred_element_type=F32)
        return carry

    lax.fori_loop(0, SECTIONS, section, 0)
    out_ref[...] = cells[...]

    for copy in wind_copies:
        copy.wait_send()
    for copy in halos + rims:
        copy.wait_send()
    for row in range(rows):
        @pl.when(row != me)
        def _():
            row_copy(row).wait_send()


def on_device(wide, concentrations, wind_speeds, rate_constants, reactants, products):
    groups, rows, columns = concentrations.shape
    assert wind_speeds.shape[2] == 1 and rows == wide and rows % CHUNK == 0
    species = groups * wide
    reactions = rate_constants.shape[0]
    wind = jnp.swapaxes(wind_speeds, 1, 2).reshape(2, 2, columns)
    dma = pltpu.SemaphoreType.DMA
    result = pl.pallas_call(
        kernel,
        out_shape=jax.ShapeDtypeStruct((species, columns), F32),
        in_specs=[pl.BlockSpec(memory_space=pltpu.VMEM)] * 5,
        out_specs=pl.BlockSpec(memory_space=pltpu.VMEM),
        scratch_shapes=[
            pltpu.VMEM((rows + 2 * HALO, groups, columns), F32),
            pltpu.VMEM((rows + HALO, groups, columns), F32),
            pltpu.VMEM((rows, groups, columns), F32),
            pltpu.VMEM((rows + 2 * HALO, 2, 2, columns), BF16),
            pltpu.VMEM((rows + 2 * HALO, 2, 2, columns), F32),
            pltpu.VMEM((wide, groups, columns), F32),
            pltpu.VMEM((species, columns), F32),
            pltpu.VMEM((2 * species, columns), BF16),
            pltpu.VMEM((2, reactions, 2 * species), BF16),
            pltpu.VMEM((species, reactions), BF16),
            pltpu.VMEM((reactions, columns), F32),
            pltpu.VMEM((reactions, columns), BF16),
            dma((wide,)), dma((wide,)), dma((2,)), dma((2,)),
            dma((2,)), dma((2,)), dma((rows,)), dma((wide,)),
        ],
        compiler_params=pltpu.CompilerParams(collective_id=0, has_side_effects=True),
        name="transport_chemistry",
    )(concentrations, wind, rate_constants.reshape(1, reactions), reactants.T, products.T)
    return result.reshape(species, 1, columns)


def solution(mesh):
    return jax.shard_map(
        functools.partial(on_device, mesh.shape["wide"]),
        mesh=mesh,
        in_specs=(
            P("wide", "narrow", None),
            P(None, None, ("narrow", "wide"), None),
            P(),
            P(),
            P(),
        ),
        out_specs=P(None, ("narrow", "wide"), None),
        check_vma=False,
    )
```

```python
import functools
import jax
import jax.numpy as jnp
from jax import lax
from jax.experimental import pallas as pl
from jax.experimental.pallas import tpu as pltpu
from jax.sharding import PartitionSpec as P

SECTIONS = 6
DIFFUSION = 0.1
CHEM_STEP = 0.02
HALO = 4
CHUNK = 4
MESH = pl.DeviceIdType.MESH
F32 = jnp.float32
BF16 = jnp.bfloat16


def minmod(first, second):
    return jnp.maximum(0.0, jnp.minimum(first, second)) + jnp.minimum(
        0.0, jnp.maximum(first, second)
    )


def coefficients(a):
    size = jnp.abs(a)
    return jnp.minimum(a, 0.0) - DIFFUSION, 0.5 * size * (1.0 - size), a >= 0.0


def sweep_rows(ext, wind):
    m = ext.shape[0] - 4
    a = 0.5 * (wind[1 : m + 2] + wind[2 : m + 3])
    jump_gain, slope_gain, forward = coefficients(a)
    jumps = ext[1:] - ext[:-1]
    slopes = minmod(jumps[:-1], jumps[1:])
    flux = (
        a * ext[1 : m + 2]
        + jump_gain * jumps[1 : m + 2]
        + slope_gain * jnp.where(forward, slopes[: m + 1], slopes[1:])
    )
    return ext[2 : m + 2] - (flux[1:] - flux[:-1])


def sweep_columns(q, wind):
    columns = q.shape[2]
    last = lax.broadcasted_iota(jnp.int32, wind.shape, 2) == columns - 1
    a = jnp.where(last, 0.0, 0.5 * (wind + pltpu.roll(wind, columns - 1, 2)))
    jump_gain, slope_gain, forward = coefficients(a)
    edge = lax.broadcasted_iota(jnp.int32, q.shape, 2) == columns - 1
    jumps = jnp.where(edge, 0.0, pltpu.roll(q, columns - 1, 2) - q)
    slopes = minmod(pltpu.roll(jumps, 1, 2), jumps)
    upwind = jnp.where(forward, slopes, pltpu.roll(slopes, columns - 1, 2))
    flux = a * q + jump_gain * jumps + slope_gain * upwind
    return q - (flux - pltpu.roll(flux, 1, 2))


def kernel(
    conc_in, wind_ref, k_in, react_in, prod_in, out_ref,
    conc_ref, k_ref, react_ref, prod_ref,
    ext, mid, done, winds, windf, incoming, cells, cells_left, picks, net, gain, rates, rates_left,
    wind_send, wind_recv, rim_send, halo_send, halo_recv, row_send, row_recv, load_sem,
):
    wide = lax.axis_size("wide")
    narrow = lax.axis_size("narrow")
    me = lax.axis_index("wide")
    slab = lax.axis_index("narrow")
    groups, rows, columns = conc_ref.shape
    species = cells.shape[0]
    reactions = react_ref.shape[1]
    lanes = k_ref.shape[1]
    above = lax.rem(slab + 1, narrow)
    below = lax.rem(slab + narrow - 1, narrow)

    barrier = pltpu.get_barrier_semaphore()
    for step in range(1, wide):
        pl.semaphore_signal(
            barrier, inc=1, device_id={"wide": lax.rem(me + step, wide)}, device_id_type=MESH
        )
    for other in (above, below):
        pl.semaphore_signal(barrier, inc=1, device_id={"narrow": other}, device_id_type=MESH)

    for place in range(HALO):
        pl.semaphore_signal(
            barrier, inc=1, device_id={"narrow": above, "wide": place}, device_id_type=MESH
        )
        pl.semaphore_signal(
            barrier,
            inc=1,
            device_id={"narrow": below, "wide": wide - 1 - place},
            device_id_type=MESH,
        )

    loads = [
        pltpu.make_async_copy(source, target, load_sem.at[index])
        for index, (source, target) in enumerate(
            (
                (conc_in, conc_ref),
                (react_in, react_ref),
                (prod_in, prod_ref),
                (k_in, k_ref),
                (wind_ref, winds.at[HALO + me]),
            )
        )
    ]
    for copy in loads:
        copy.start()

    low_rim = (wide - 1 - me + HALO) // wide
    high_rim = (me + HALO) // wide
    pl.semaphore_wait(barrier, wide + 1 + wide * (low_rim + high_rim))

    def wind_copy(slot, send, **device):
        return pltpu.make_async_remote_copy(
            src_ref=wind_ref,
            dst_ref=winds.at[slot],
            send_sem=send,
            recv_sem=wind_recv.at[slot],
            device_id=device,
            device_id_type=MESH,
        )

    wind_copies = [
        wind_copy(HALO + me, wind_send.at[step], wide=lax.rem(me + step, wide))
        for step in range(1, wide)
    ]

    def rim_copies(act):
        @pl.when(me < HALO)
        def _():
            for step in range(wide):
                act(
                    wind_copy(
                        HALO + rows + me,
                        rim_send.at[0, step],
                        narrow=below,
                        wide=lax.rem(me + step, wide),
                    )
                )

        @pl.when(me >= wide - HALO)
        def _():
            for step in range(wide):
                act(
                    wind_copy(
                        me - (wide - HALO),
                        rim_send.at[1, step],
                        narrow=above,
                        wide=lax.rem(me + step, wide),
                    )
                )

    def halo_copies(buffer, send, recv):
        up = pltpu.make_async_remote_copy(
            src_ref=buffer.at[pl.ds(rows, HALO)],
            dst_ref=buffer.at[pl.ds(0, HALO)],
            send_sem=send.at[0],
            recv_sem=recv.at[0],
            device_id={"narrow": above},
            device_id_type=MESH,
        )
        down = pltpu.make_async_remote_copy(
            src_ref=buffer.at[pl.ds(HALO, HALO)],
            dst_ref=buffer.at[pl.ds(HALO + rows, HALO)],
            send_sem=send.at[1],
            recv_sem=recv.at[1],
            device_id={"narrow": below},
            device_id_type=MESH,
        )
        return up, down

    for copy in wind_copies:
        copy.start()
    rim_copies(lambda copy: copy.start())

    loads[0].wait()
    ext[HALO : HALO + rows] = jnp.swapaxes(conc_ref[...], 0, 1)
    halos = halo_copies(ext, halo_send, halo_recv)
    for copy in halos:
        copy.start()

    for copy in loads[1:]:
        copy.wait()
    ids = lax.broadcasted_iota(jnp.int32, (species, reactions), 0)

    def one_hot(ref, which):
        return jnp.where(ids == ref[which : which + 1, :], 1.0, 0.0)

    first, second = one_hot(react_ref, 0), one_hot(react_ref, 1)
    net[...] = (one_hot(prod_ref, 0) + one_hot(prod_ref, 1) - first - second).astype(BF16)
    for index, table in enumerate((first, second)):
        picks[index] = jnp.transpose(table).astype(BF16)
    for part in range(reactions // lanes):
        constants = CHEM_STEP * k_ref[part : part + 1, :]
        gain[part * lanes : (part + 1) * lanes] = jnp.transpose(
            jnp.broadcast_to(constants, (columns, lanes))
        )
    cells_left[...] = jnp.zeros_like(cells_left)
    rates_left[...] = jnp.zeros_like(rates_left)

    def wind_arrival(slot):
        wind_copy(slot, wind_send.at[0], wide=lax.rem(me + 1, wide)).wait_recv()

    for source in range(wide):
        @pl.when(source != me)
        def _():
            wind_arrival(HALO + source)

    windf[HALO : HALO + rows] = winds[HALO : HALO + rows].astype(F32)

    def wind_of(substep, direction, start, count):
        return windf[start : start + count, substep, direction : direction + 1, :]

    def first_substep(o):
        swept = sweep_rows(ext[o : o + CHUNK + 4], wind_of(0, 0, o, CHUNK + 4))
        mid[o : o + CHUNK] = sweep_columns(swept, wind_of(0, 1, o + 2, CHUNK))

    def second_substep(g):
        swept = sweep_rows(mid[g : g + CHUNK + 4], wind_of(1, 0, g + 2, CHUNK + 4))
        done[g : g + CHUNK] = sweep_columns(swept, wind_of(1, 1, g + 4, CHUNK))

    def row_copy(row):
        return pltpu.make_async_remote_copy(
            src_ref=done.at[row],
            dst_ref=incoming.at[me],
            send_sem=row_send.at[row],
            recv_sem=row_recv.at[me],
            device_id={"wide": row},
            device_id_type=MESH,
        )

    def send_row(row):
        @pl.when(row != me)
        def _():
            row_copy(row).start()

    inner = rows - 2 * HALO
    for o in range(HALO, rows, CHUNK):
        first_substep(o)
    for g in range(HALO, rows - HALO, CHUNK):
        second_substep(g)
    for k in range(inner):
        send_row(HALO + lax.rem(me + k, inner))

    for slot in range(HALO):
        wind_arrival(slot)
        wind_arrival(HALO + rows + slot)
    for copy in halos:
        copy.wait_recv()
    windf[0:HALO] = winds[0:HALO].astype(F32)
    windf[HALO + rows :] = winds[HALO + rows :].astype(F32)
    for o in (0, rows):
        first_substep(o)
    for g in (0, rows - HALO):
        second_substep(g)
    for k in range(2 * HALO):
        index = lax.rem(me + k, 2 * HALO)
        send_row(index + inner * (index // HALO))

    incoming[me] = done[me]
    for source in range(wide):
        @pl.when(source != me)
        def _():
            pltpu.make_async_remote_copy(
                src_ref=done.at[source],
                dst_ref=incoming.at[source],
                send_sem=row_send.at[source],
                recv_sem=row_recv.at[source],
                device_id={"wide": source},
                device_id_type=MESH,
            ).wait_recv()

    for source in range(wide):
        cells[source * groups : (source + 1) * groups] = incoming[source]

    block = species

    def section(_, carry):
        q = cells[...]
        wanted = q + cells_left[...]
        high = wanted.astype(BF16)
        cells_left[...] = wanted - high.astype(F32)
        for start in range(0, reactions, block):
            span = pl.ds(start, block)
            one = jnp.dot(picks[0, span, :], high, preferred_element_type=F32)
            two = jnp.dot(picks[1, span, :], high, preferred_element_type=F32)
            rate = gain[span, :] * one * two + rates_left[span, :]
            rounded = rate.astype(BF16)
            rates_left[span, :] = rate - rounded.astype(F32)
            rates[span, :] = rounded
        cells[...] = q + jnp.dot(net[...], rates[...], preferred_element_type=F32)
        return carry

    lax.fori_loop(0, SECTIONS, section, 0)
    parts = columns // lanes
    for part in range(parts):
        out_ref[pl.ds(part, species, stride=parts), :] = cells[:, part * lanes : (part + 1) * lanes]

    for copy in wind_copies:
        copy.wait_send()
    rim_copies(lambda copy: copy.wait_send())
    for copy in halos:
        copy.wait_send()
    for row in range(rows):
        @pl.when(row != me)
        def _():
            row_copy(row).wait_send()


def on_device(wide, concentrations, wind_speeds, rate_constants, reactants, products):
    groups, rows, columns = concentrations.shape
    assert wind_speeds.shape[2] == 1 and 2 * HALO <= rows and rows == wide and rows % CHUNK == 0
    species = groups * wide
    reactions = rate_constants.shape[0]
    wind = jnp.swapaxes(wind_speeds, 1, 2).reshape(2, 2, columns)
    lanes = 128
    dma = pltpu.SemaphoreType.DMA
    result = pl.pallas_call(
        kernel,
        out_shape=jax.ShapeDtypeStruct((species * columns // lanes, lanes), F32),
        in_specs=[pl.BlockSpec(memory_space=pl.ANY)] * 5,
        out_specs=pl.BlockSpec(memory_space=pltpu.VMEM),
        scratch_shapes=[
            pltpu.VMEM((groups, rows, columns), F32),
            pltpu.VMEM((reactions // lanes, lanes), F32),
            pltpu.VMEM((2, reactions), jnp.int32),
            pltpu.VMEM((2, reactions), jnp.int32),
            pltpu.VMEM((rows + 2 * HALO, groups, columns), F32),
            pltpu.VMEM((rows + HALO, groups, columns), F32),
            pltpu.VMEM((rows, groups, columns), F32),
            pltpu.VMEM((rows + 2 * HALO, 2, 2, columns), BF16),
            pltpu.VMEM((rows + 2 * HALO, 2, 2, columns), F32),
            pltpu.VMEM((wide, groups, columns), F32),
            pltpu.VMEM((species, columns), F32),
            pltpu.VMEM((species, columns), F32),
            pltpu.VMEM((2, reactions, species), BF16),
            pltpu.VMEM((species, reactions), BF16),
            pltpu.VMEM((reactions, columns), F32),
            pltpu.VMEM((reactions, columns), BF16),
            pltpu.VMEM((reactions, columns), F32),
            dma((wide,)), dma((rows + 2 * HALO,)), dma((2, wide)),
            dma((2,)), dma((2,)), dma((rows,)), dma((wide,)), dma((5,)),
        ],
        compiler_params=pltpu.CompilerParams(collective_id=0, has_side_effects=True),
        name="transport_chemistry",
    )(concentrations, wind, rate_constants.reshape(-1, lanes), reactants.T, products.T)
    return result.reshape(species, 1, columns)


def solution(mesh):
    return jax.shard_map(
        functools.partial(on_device, mesh.shape["wide"]),
        mesh=mesh,
        in_specs=(
            P("wide", "narrow", None),
            P(None, None, ("narrow", "wide"), None),
            P(),
            P(),
            P(),
        ),
        out_specs=P(None, ("narrow", "wide"), None),
        check_vma=False,
    )
```

```python
import functools
import jax
import jax.numpy as jnp
from jax import lax
from jax.experimental import pallas as pl
from jax.experimental.pallas import tpu as pltpu
from jax.sharding import PartitionSpec as P

SECTIONS = 6
DIFFUSION = 0.1
CHEM_STEP = 0.02
HALO = 4
CHUNK = 4
MESH = pl.DeviceIdType.MESH
F32 = jnp.float32
BF16 = jnp.bfloat16


MIDDLE = 1.05
REACH = 0.95
TOP_CODE = 32760.0


def to_codes(scaled):
    return jnp.round(scaled).astype(jnp.int32).astype(jnp.int16)


def from_codes(codes):
    return codes.astype(jnp.int32).astype(F32)


def minmod(first, second):
    return jnp.maximum(0.0, jnp.minimum(first, second)) + jnp.minimum(
        0.0, jnp.maximum(first, second)
    )


def coefficients(a):
    size = jnp.abs(a)
    return jnp.minimum(a, 0.0) - DIFFUSION, 0.5 * size * (1.0 - size), a >= 0.0


def sweep_rows(ext, wind):
    m = ext.shape[0] - 4
    a = 0.5 * (wind[1 : m + 2] + wind[2 : m + 3])
    jump_gain, slope_gain, forward = coefficients(a)
    jumps = ext[1:] - ext[:-1]
    slopes = minmod(jumps[:-1], jumps[1:])
    flux = (
        a * ext[1 : m + 2]
        + jump_gain * jumps[1 : m + 2]
        + slope_gain * jnp.where(forward, slopes[: m + 1], slopes[1:])
    )
    return ext[2 : m + 2] - (flux[1:] - flux[:-1])


def sweep_columns(q, wind):
    columns = q.shape[2]
    last = lax.broadcasted_iota(jnp.int32, wind.shape, 2) == columns - 1
    a = jnp.where(last, 0.0, 0.5 * (wind + pltpu.roll(wind, columns - 1, 2)))
    jump_gain, slope_gain, forward = coefficients(a)
    edge = lax.broadcasted_iota(jnp.int32, q.shape, 2) == columns - 1
    jumps = jnp.where(edge, 0.0, pltpu.roll(q, columns - 1, 2) - q)
    slopes = minmod(pltpu.roll(jumps, 1, 2), jumps)
    upwind = jnp.where(forward, slopes, pltpu.roll(slopes, columns - 1, 2))
    flux = a * q + jump_gain * jumps + slope_gain * upwind
    return q - (flux - pltpu.roll(flux, 1, 2))


def kernel(
    conc_in, wind_ref, k_in, react_in, prod_in, out_ref,
    conc_ref, k_ref, react_ref, prod_ref,
    ext, mid, rims_out, rims_in, codes, tops, winds, windf, codes_in, tops_in, cells, cells_left, picks, net, gain, rates, rates_left,
    wind_send, wind_recv, rim_send, halo_send, halo_recv, row_send, row_recv, load_sem,
):
    wide = lax.axis_size("wide")
    narrow = lax.axis_size("narrow")
    me = lax.axis_index("wide")
    slab = lax.axis_index("narrow")
    groups, rows, columns = conc_ref.shape
    species = cells.shape[0]
    reactions = react_ref.shape[1]
    lanes = k_ref.shape[1]
    above = lax.rem(slab + 1, narrow)
    below = lax.rem(slab + narrow - 1, narrow)

    barrier = pltpu.get_barrier_semaphore()
    for step in range(1, wide):
        pl.semaphore_signal(
            barrier, inc=1, device_id={"wide": lax.rem(me + step, wide)}, device_id_type=MESH
        )
    for other in (above, below):
        pl.semaphore_signal(barrier, inc=1, device_id={"narrow": other}, device_id_type=MESH)

    for place in range(HALO):
        pl.semaphore_signal(
            barrier, inc=1, device_id={"narrow": above, "wide": place}, device_id_type=MESH
        )
        pl.semaphore_signal(
            barrier,
            inc=1,
            device_id={"narrow": below, "wide": wide - 1 - place},
            device_id_type=MESH,
        )

    loads = [
        pltpu.make_async_copy(source, target, load_sem.at[index])
        for index, (source, target) in enumerate(
            (
                (conc_in, conc_ref),
                (react_in, react_ref),
                (prod_in, prod_ref),
                (k_in, k_ref),
                (wind_ref, winds.at[HALO + me]),
            )
        )
    ]
    for copy in loads:
        copy.start()

    low_rim = (wide - 1 - me + HALO) // wide
    high_rim = (me + HALO) // wide
    pl.semaphore_wait(barrier, wide + 1 + wide * (low_rim + high_rim))

    def wind_copy(slot, send, **device):
        return pltpu.make_async_remote_copy(
            src_ref=wind_ref,
            dst_ref=winds.at[slot],
            send_sem=send,
            recv_sem=wind_recv.at[slot],
            device_id=device,
            device_id_type=MESH,
        )

    wind_copies = [
        wind_copy(HALO + me, wind_send.at[step], wide=lax.rem(me + step, wide))
        for step in range(1, wide)
    ]

    def rim_copies(act):
        @pl.when(me < HALO)
        def _():
            for step in range(wide):
                act(
                    wind_copy(
                        HALO + rows + me,
                        rim_send.at[0, step],
                        narrow=below,
                        wide=lax.rem(me + step, wide),
                    )
                )

        @pl.when(me >= wide - HALO)
        def _():
            for step in range(wide):
                act(
                    wind_copy(
                        me - (wide - HALO),
                        rim_send.at[1, step],
                        narrow=above,
                        wide=lax.rem(me + step, wide),
                    )
                )

    halos = [
        pltpu.make_async_remote_copy(
            src_ref=rims_out.at[side],
            dst_ref=rims_in.at[side],
            send_sem=halo_send.at[side],
            recv_sem=halo_recv.at[side],
            device_id={"narrow": other},
            device_id_type=MESH,
        )
        for side, other in enumerate((above, below))
    ]

    for copy in wind_copies:
        copy.start()
    rim_copies(lambda copy: copy.start())

    loads[0].wait()
    turned = jnp.swapaxes(conc_ref[...], 0, 1)
    ext[HALO : HALO + rows] = turned
    for side, rim in enumerate((turned[rows - HALO :], turned[:HALO])):
        rims_out[side] = to_codes((rim - MIDDLE) * (TOP_CODE / REACH))
    for copy in halos:
        copy.start()

    for copy in loads[1:]:
        copy.wait()
    ids = lax.broadcasted_iota(jnp.int32, (species, reactions), 0)

    def one_hot(ref, which):
        return jnp.where(ids == ref[which : which + 1, :], 1.0, 0.0)

    first, second = one_hot(react_ref, 0), one_hot(react_ref, 1)
    net[...] = (one_hot(prod_ref, 0) + one_hot(prod_ref, 1) - first - second).astype(BF16)
    for index, table in enumerate((first, second)):
        picks[index] = jnp.transpose(table).astype(BF16)
    for part in range(reactions // lanes):
        constants = CHEM_STEP * k_ref[part : part + 1, :]
        gain[part * lanes : (part + 1) * lanes] = jnp.transpose(
            jnp.broadcast_to(constants, (columns, lanes))
        )
    cells_left[...] = jnp.zeros_like(cells_left)
    rates_left[...] = jnp.zeros_like(rates_left)

    def wind_arrival(slot):
        wind_copy(slot, wind_send.at[0], wide=lax.rem(me + 1, wide)).wait_recv()

    for source in range(wide):
        @pl.when(source != me)
        def _():
            wind_arrival(HALO + source)

    windf[HALO : HALO + rows] = winds[HALO : HALO + rows].astype(F32)

    def wind_of(substep, direction, start, count):
        return windf[start : start + count, substep, direction : direction + 1, :]

    def first_substep(o):
        swept = sweep_rows(ext[o : o + CHUNK + 4], wind_of(0, 0, o, CHUNK + 4))
        mid[o : o + CHUNK] = sweep_columns(swept, wind_of(0, 1, o + 2, CHUNK))

    def second_substep(g):
        swept = sweep_rows(mid[g : g + CHUNK + 4], wind_of(1, 0, g + 2, CHUNK + 4))
        value = sweep_columns(swept, wind_of(1, 1, g + 4, CHUNK))
        top = jnp.maximum(jnp.max(jnp.abs(value), axis=1, keepdims=True), 1e-30)
        codes[g : g + CHUNK] = to_codes(value * (TOP_CODE / top))
        tops[g : g + CHUNK] = top * (1.0 / TOP_CODE)

    def row_copies(row, source):
        return [
            pltpu.make_async_remote_copy(
                src_ref=here.at[row],
                dst_ref=there.at[source],
                send_sem=row_send.at[index, row],
                recv_sem=row_recv.at[index, source],
                device_id={"wide": row},
                device_id_type=MESH,
            )
            for index, (here, there) in enumerate(((codes, codes_in), (tops, tops_in)))
        ]

    def send_row(row):
        @pl.when(row != me)
        def _():
            for copy in row_copies(row, me):
                copy.start()

    inner = rows - 2 * HALO
    for o in range(HALO, rows, CHUNK):
        first_substep(o)
    for g in range(HALO, rows - HALO, CHUNK):
        second_substep(g)
    for k in range(inner):
        send_row(HALO + lax.rem(me + k, inner))

    for slot in range(HALO):
        wind_arrival(slot)
        wind_arrival(HALO + rows + slot)
    for copy in halos:
        copy.wait_recv()
    for side, start in enumerate((0, HALO + rows)):
        ext[start : start + HALO] = from_codes(rims_in[side]) * (REACH / TOP_CODE) + MIDDLE
    windf[0:HALO] = winds[0:HALO].astype(F32)
    windf[HALO + rows :] = winds[HALO + rows :].astype(F32)
    for o in (0, rows):
        first_substep(o)
    for g in (0, rows - HALO):
        second_substep(g)
    for k in range(2 * HALO):
        index = lax.rem(me + k, 2 * HALO)
        send_row(index + inner * (index // HALO))

    codes_in[me] = codes[me]
    tops_in[me] = tops[me]
    for source in range(wide):
        @pl.when(source != me)
        def _():
            for copy in row_copies(source, source):
                copy.wait_recv()

    for source in range(wide):
        cells[source * groups : (source + 1) * groups] = (
            from_codes(codes_in[source]) * tops_in[source]
        )

    block = species

    def section(_, carry):
        q = cells[...]
        wanted = q + cells_left[...]
        high = wanted.astype(BF16)
        cells_left[...] = wanted - high.astype(F32)
        for start in range(0, reactions, block):
            span = pl.ds(start, block)
            one = jnp.dot(picks[0, span, :], high, preferred_element_type=F32)
            two = jnp.dot(picks[1, span, :], high, preferred_element_type=F32)
            rate = gain[span, :] * one * two + rates_left[span, :]
            rounded = rate.astype(BF16)
            rates_left[span, :] = rate - rounded.astype(F32)
            rates[span, :] = rounded
        cells[...] = q + jnp.dot(net[...], rates[...], preferred_element_type=F32)
        return carry

    lax.fori_loop(0, SECTIONS, section, 0)
    parts = columns // lanes
    for part in range(parts):
        out_ref[pl.ds(part, species, stride=parts), :] = cells[:, part * lanes : (part + 1) * lanes]

    for copy in wind_copies:
        copy.wait_send()
    rim_copies(lambda copy: copy.wait_send())
    for copy in halos:
        copy.wait_send()
    for row in range(rows):
        @pl.when(row != me)
        def _():
            for copy in row_copies(row, me):
                copy.wait_send()


def on_device(wide, concentrations, wind_speeds, rate_constants, reactants, products):
    groups, rows, columns = concentrations.shape
    assert wind_speeds.shape[2] == 1 and 2 * HALO <= rows and rows == wide and rows % CHUNK == 0
    species = groups * wide
    reactions = rate_constants.shape[0]
    wind = jnp.swapaxes(wind_speeds, 1, 2).reshape(2, 2, columns)
    lanes = 128
    dma = pltpu.SemaphoreType.DMA
    result = pl.pallas_call(
        kernel,
        out_shape=jax.ShapeDtypeStruct((species * columns // lanes, lanes), F32),
        in_specs=[pl.BlockSpec(memory_space=pl.ANY)] * 5,
        out_specs=pl.BlockSpec(memory_space=pltpu.VMEM),
        scratch_shapes=[
            pltpu.VMEM((groups, rows, columns), F32),
            pltpu.VMEM((reactions // lanes, lanes), F32),
            pltpu.VMEM((2, reactions), jnp.int32),
            pltpu.VMEM((2, reactions), jnp.int32),
            pltpu.VMEM((rows + 2 * HALO, groups, columns), F32),
            pltpu.VMEM((rows + HALO, groups, columns), F32),
            pltpu.VMEM((2, HALO, groups, columns), jnp.int16),
            pltpu.VMEM((2, HALO, groups, columns), jnp.int16),
            pltpu.VMEM((rows, groups, columns), jnp.int16),
            pltpu.VMEM((rows, 1, columns), F32),
            pltpu.VMEM((rows + 2 * HALO, 2, 2, columns), BF16),
            pltpu.VMEM((rows + 2 * HALO, 2, 2, columns), F32),
            pltpu.VMEM((wide, groups, columns), jnp.int16),
            pltpu.VMEM((wide, 1, columns), F32),
            pltpu.VMEM((species, columns), F32),
            pltpu.VMEM((species, columns), F32),
            pltpu.VMEM((2, reactions, species), BF16),
            pltpu.VMEM((species, reactions), BF16),
            pltpu.VMEM((reactions, columns), F32),
            pltpu.VMEM((reactions, columns), BF16),
            pltpu.VMEM((reactions, columns), F32),
            dma((wide,)), dma((rows + 2 * HALO,)), dma((2, wide)),
            dma((2,)), dma((2,)), dma((2, rows)), dma((2, wide)), dma((5,)),
        ],
        compiler_params=pltpu.CompilerParams(collective_id=0, has_side_effects=True),
        name="transport_chemistry",
    )(concentrations, wind, rate_constants.reshape(-1, lanes), reactants.T, products.T)
    return result.reshape(species, 1, columns)


def solution(mesh):
    return jax.shard_map(
        functools.partial(on_device, mesh.shape["wide"]),
        mesh=mesh,
        in_specs=(
            P("wide", "narrow", None),
            P(None, None, ("narrow", "wide"), None),
            P(),
            P(),
            P(),
        ),
        out_specs=P(None, ("narrow", "wide"), None),
        check_vma=False,
    )
```

```python
import functools
import jax
import jax.numpy as jnp
from jax import lax
from jax.experimental import pallas as pl
from jax.experimental.pallas import tpu as pltpu
from jax.sharding import PartitionSpec as P

SECTIONS = 6
DIFFUSION = 0.1
CHEM_STEP = 0.02
HALO = 4
CHUNK = 4
MESH = pl.DeviceIdType.MESH
F32 = jnp.float32
BF16 = jnp.bfloat16


MIDDLE = 1.05
REACH = 0.95
TOP_CODE = 32760.0


def to_codes(scaled):
    return jnp.round(scaled).astype(jnp.int32).astype(jnp.int16)


def from_codes(codes):
    return codes.astype(jnp.int32).astype(F32)


def minmod(first, second):
    return jnp.maximum(0.0, jnp.minimum(first, second)) + jnp.minimum(
        0.0, jnp.maximum(first, second)
    )


def coefficients(a):
    size = jnp.abs(a)
    return jnp.minimum(a, 0.0) - DIFFUSION, 0.5 * size * (1.0 - size), a >= 0.0


def sweep_rows(ext, wind):
    m = ext.shape[0] - 4
    a = 0.5 * (wind[1 : m + 2] + wind[2 : m + 3])
    jump_gain, slope_gain, forward = coefficients(a)
    jumps = ext[1:] - ext[:-1]
    slopes = minmod(jumps[:-1], jumps[1:])
    flux = (
        a * ext[1 : m + 2]
        + jump_gain * jumps[1 : m + 2]
        + slope_gain * jnp.where(forward, slopes[: m + 1], slopes[1:])
    )
    return ext[2 : m + 2] - (flux[1:] - flux[:-1])


def sweep_columns(q, wind):
    columns = q.shape[2]
    last = lax.broadcasted_iota(jnp.int32, wind.shape, 2) == columns - 1
    a = jnp.where(last, 0.0, 0.5 * (wind + pltpu.roll(wind, columns - 1, 2)))
    jump_gain, slope_gain, forward = coefficients(a)
    edge = lax.broadcasted_iota(jnp.int32, q.shape, 2) == columns - 1
    jumps = jnp.where(edge, 0.0, pltpu.roll(q, columns - 1, 2) - q)
    slopes = minmod(pltpu.roll(jumps, 1, 2), jumps)
    upwind = jnp.where(forward, slopes, pltpu.roll(slopes, columns - 1, 2))
    flux = a * q + jump_gain * jumps + slope_gain * upwind
    return q - (flux - pltpu.roll(flux, 1, 2))


def kernel(
    conc_in, wind_in, k_in, react_in, prod_in, out_ref,
    conc_ref, k_ref, react_ref, prod_ref,
    ext, mid, rims_out, rims_in, codes, tops, winds, windf, codes_in, tops_in, cells, cells_left, picks, net, gain, rates, rates_left,
    wind_send, wind_recv, rim_send, halo_send, halo_recv, row_send, row_recv, load_sem,
):
    wide = lax.axis_size("wide")
    narrow = lax.axis_size("narrow")
    me = lax.axis_index("wide")
    slab = lax.axis_index("narrow")
    groups, rows, columns = conc_ref.shape
    species = cells.shape[0]
    reactions = react_ref.shape[1]
    lanes = k_ref.shape[1]
    above = lax.rem(slab + 1, narrow)
    below = lax.rem(slab + narrow - 1, narrow)

    barrier = pltpu.get_barrier_semaphore()
    for step in range(1, wide):
        pl.semaphore_signal(
            barrier, inc=1, device_id={"wide": lax.rem(me + step, wide)}, device_id_type=MESH
        )
    for other in (above, below):
        pl.semaphore_signal(barrier, inc=1, device_id={"narrow": other}, device_id_type=MESH)

    for place in range(HALO):
        pl.semaphore_signal(
            barrier, inc=1, device_id={"narrow": above, "wide": place}, device_id_type=MESH
        )
        pl.semaphore_signal(
            barrier,
            inc=1,
            device_id={"narrow": below, "wide": wide - 1 - place},
            device_id_type=MESH,
        )

    loads = [
        pltpu.make_async_copy(source, target, load_sem.at[index])
        for index, (source, target) in enumerate(
            (
                (conc_in, conc_ref),
                (react_in, react_ref),
                (prod_in, prod_ref),
                (k_in, k_ref),
                (wind_in, winds.at[HALO + me]),
            )
        )
    ]
    for copy in loads[::-1]:
        copy.start()

    low_rim = (wide - 1 - me + HALO) // wide
    high_rim = (me + HALO) // wide
    pl.semaphore_wait(barrier, wide + 1 + wide * (low_rim + high_rim))

    def wind_copy(slot, send, **device):
        return pltpu.make_async_remote_copy(
            src_ref=winds.at[HALO + me],
            dst_ref=winds.at[slot],
            send_sem=send,
            recv_sem=wind_recv.at[slot],
            device_id=device,
            device_id_type=MESH,
        )

    wind_copies = [
        wind_copy(HALO + me, wind_send.at[step], wide=lax.rem(me + step, wide))
        for step in range(1, wide)
    ]

    def rim_copies(act):
        @pl.when(me < HALO)
        def _():
            for step in range(wide):
                act(
                    wind_copy(
                        HALO + rows + me,
                        rim_send.at[0, step],
                        narrow=below,
                        wide=lax.rem(me + step, wide),
                    )
                )

        @pl.when(me >= wide - HALO)
        def _():
            for step in range(wide):
                act(
                    wind_copy(
                        me - (wide - HALO),
                        rim_send.at[1, step],
                        narrow=above,
                        wide=lax.rem(me + step, wide),
                    )
                )

    halos = [
        pltpu.make_async_remote_copy(
            src_ref=rims_out.at[side],
            dst_ref=rims_in.at[side],
            send_sem=halo_send.at[side],
            recv_sem=halo_recv.at[side],
            device_id={"narrow": other},
            device_id_type=MESH,
        )
        for side, other in enumerate((above, below))
    ]

    loads[-1].wait()
    for copy in wind_copies:
        copy.start()
    rim_copies(lambda copy: copy.start())

    loads[0].wait()
    turned = jnp.swapaxes(conc_ref[...], 0, 1)
    ext[HALO : HALO + rows] = turned
    for side, rim in enumerate((turned[rows - HALO :], turned[:HALO])):
        rims_out[side] = to_codes((rim - MIDDLE) * (TOP_CODE / REACH))
    for copy in halos:
        copy.start()

    for copy in loads[1:-1]:
        copy.wait()
    ids = lax.broadcasted_iota(jnp.int32, (species, reactions), 0)

    def one_hot(ref, which):
        return jnp.where(ids == ref[which : which + 1, :], 1.0, 0.0)

    first, second = one_hot(react_ref, 0), one_hot(react_ref, 1)
    net[...] = (one_hot(prod_ref, 0) + one_hot(prod_ref, 1) - first - second).astype(BF16)
    for index, table in enumerate((first, second)):
        picks[index] = jnp.transpose(table).astype(BF16)
    for part in range(reactions // lanes):
        constants = CHEM_STEP * k_ref[part : part + 1, :]
        gain[part * lanes : (part + 1) * lanes] = jnp.transpose(
            jnp.broadcast_to(constants, (columns, lanes))
        )
    cells_left[...] = jnp.zeros_like(cells_left)
    rates_left[...] = jnp.zeros_like(rates_left)

    def wind_arrival(slot):
        wind_copy(slot, wind_send.at[0], wide=lax.rem(me + 1, wide)).wait_recv()

    for step in range(1, wide):
        wind_arrival(HALO + lax.rem(me + step, wide))

    windf[HALO : HALO + rows] = winds[HALO : HALO + rows].astype(F32)

    def wind_of(substep, direction, start, count):
        return windf[start : start + count, substep, direction : direction + 1, :]

    def first_substep(o):
        swept = sweep_rows(ext[o : o + CHUNK + 4], wind_of(0, 0, o, CHUNK + 4))
        mid[o : o + CHUNK] = sweep_columns(swept, wind_of(0, 1, o + 2, CHUNK))

    def second_substep(g):
        swept = sweep_rows(mid[g : g + CHUNK + 4], wind_of(1, 0, g + 2, CHUNK + 4))
        value = sweep_columns(swept, wind_of(1, 1, g + 4, CHUNK))
        top = jnp.maximum(jnp.max(jnp.abs(value), axis=1, keepdims=True), 1e-30)
        codes[g : g + CHUNK] = to_codes(value * (TOP_CODE / top))
        tops[g : g + CHUNK] = top * (1.0 / TOP_CODE)

    def row_copies(row, source):
        return [
            pltpu.make_async_remote_copy(
                src_ref=here.at[row],
                dst_ref=there.at[source],
                send_sem=row_send.at[index, row],
                recv_sem=row_recv.at[index, source],
                device_id={"wide": row},
                device_id_type=MESH,
            )
            for index, (here, there) in enumerate(((codes, codes_in), (tops, tops_in)))
        ]

    others = [lax.rem(me + step, wide) for step in range(1, wide)]

    for o in range(HALO, rows, CHUNK):
        first_substep(o)
    for g in range(HALO, rows - HALO, CHUNK):
        second_substep(g)

    for slot in range(HALO):
        wind_arrival(slot)
        wind_arrival(HALO + rows + slot)
    for copy in halos:
        copy.wait_recv()
    for side, start in enumerate((0, HALO + rows)):
        ext[start : start + HALO] = from_codes(rims_in[side]) * (REACH / TOP_CODE) + MIDDLE
    windf[0:HALO] = winds[0:HALO].astype(F32)
    windf[HALO + rows :] = winds[HALO + rows :].astype(F32)
    for o in (0, rows):
        first_substep(o)
    for g in (0, rows - HALO):
        second_substep(g)
    for other in others:
        for copy in row_copies(other, me):
            copy.start()
    codes_in[me] = codes[me]
    tops_in[me] = tops[me]
    for other in others:
        for copy in row_copies(other, other):
            copy.wait_recv()

    for source in range(wide):
        cells[source * groups : (source + 1) * groups] = (
            from_codes(codes_in[source]) * tops_in[source]
        )

    block = species

    def section(_, carry):
        q = cells[...]
        wanted = q + cells_left[...]
        high = wanted.astype(BF16)
        cells_left[...] = wanted - high.astype(F32)
        for start in range(0, reactions, block):
            span = pl.ds(start, block)
            one = jnp.dot(picks[0, span, :], high, preferred_element_type=F32)
            two = jnp.dot(picks[1, span, :], high, preferred_element_type=F32)
            rate = gain[span, :] * one * two + rates_left[span, :]
            rounded = rate.astype(BF16)
            rates_left[span, :] = rate - rounded.astype(F32)
            rates[span, :] = rounded
        cells[...] = q + jnp.dot(net[...], rates[...], preferred_element_type=F32)
        return carry

    lax.fori_loop(0, SECTIONS, section, 0)
    parts = columns // lanes
    for part in range(parts):
        out_ref[pl.ds(part, species, stride=parts), :] = cells[:, part * lanes : (part + 1) * lanes]

    for copy in wind_copies:
        copy.wait_send()
    rim_copies(lambda copy: copy.wait_send())
    for copy in halos:
        copy.wait_send()
    for other in others:
        for copy in row_copies(other, me):
            copy.wait_send()


def place_kernel(result_ref, out_ref, sem):
    copy = pltpu.make_async_copy(result_ref, out_ref, sem)
    copy.start()
    copy.wait()


def on_device(wide, concentrations, wind_speeds, rate_constants, reactants, products):
    groups, rows, columns = concentrations.shape
    assert wind_speeds.shape[2] == 1 and 2 * HALO <= rows and rows == wide and rows % CHUNK == 0
    species = groups * wide
    reactions = rate_constants.shape[0]
    wind = jnp.swapaxes(wind_speeds, 1, 2).reshape(2, 2, columns)
    lanes = 128
    dma = pltpu.SemaphoreType.DMA
    inputs = (
        concentrations,
        wind,
        rate_constants.reshape(-1, lanes),
        reactants.T,
        products.T,
    )
    result = pl.pallas_call(
        kernel,
        out_shape=jax.ShapeDtypeStruct((species * columns // lanes, lanes), F32),
        in_specs=[pl.BlockSpec(memory_space=pltpu.HBM)] * 5,
        out_specs=pl.BlockSpec(memory_space=pltpu.VMEM),
        scratch_shapes=[
            pltpu.VMEM((groups, rows, columns), F32),
            pltpu.VMEM((reactions // lanes, lanes), F32),
            pltpu.VMEM((2, reactions), jnp.int32),
            pltpu.VMEM((2, reactions), jnp.int32),
            pltpu.VMEM((rows + 2 * HALO, groups, columns), F32),
            pltpu.VMEM((rows + HALO, groups, columns), F32),
            pltpu.VMEM((2, HALO, groups, columns), jnp.int16),
            pltpu.VMEM((2, HALO, groups, columns), jnp.int16),
            pltpu.VMEM((rows, groups, columns), jnp.int16),
            pltpu.VMEM((rows, 1, columns), F32),
            pltpu.VMEM((rows + 2 * HALO, 2, 2, columns), BF16),
            pltpu.VMEM((rows + 2 * HALO, 2, 2, columns), F32),
            pltpu.VMEM((wide, groups, columns), jnp.int16),
            pltpu.VMEM((wide, 1, columns), F32),
            pltpu.VMEM((species, columns), F32),
            pltpu.VMEM((species, columns), F32),
            pltpu.VMEM((2, reactions, species), BF16),
            pltpu.VMEM((species, reactions), BF16),
            pltpu.VMEM((reactions, columns), F32),
            pltpu.VMEM((reactions, columns), BF16),
            pltpu.VMEM((reactions, columns), F32),
            dma((wide,)), dma((rows + 2 * HALO,)), dma((2, wide)),
            dma((2,)), dma((2,)), dma((2, rows)), dma((2, wide)), dma((5,)),
        ],
        compiler_params=pltpu.CompilerParams(
            collective_id=0, has_side_effects=True, vmem_limit_bytes=24 * 2**20
        ),
        name="transport_chemistry",
    )(*[pltpu.with_memory_space_constraint(each, pltpu.HBM) for each in inputs])
    result = pl.pallas_call(
        place_kernel,
        out_shape=jax.ShapeDtypeStruct(result.shape, F32),
        in_specs=[pl.BlockSpec(memory_space=pltpu.VMEM)],
        out_specs=pl.BlockSpec(memory_space=pl.ANY),
        scratch_shapes=[dma(())],
        compiler_params=pltpu.CompilerParams(vmem_limit_bytes=2**20),
        name="place",
    )(result)
    return result.reshape(species, 1, columns)


def solution(mesh):
    return jax.shard_map(
        functools.partial(on_device, mesh.shape["wide"]),
        mesh=mesh,
        in_specs=(
            P("wide", "narrow", None),
            P(None, None, ("narrow", "wide"), None),
            P(),
            P(),
            P(),
        ),
        out_specs=P(None, ("narrow", "wide"), None),
        check_vma=False,
    )
```

```python
import functools
import jax
import jax.numpy as jnp
from jax import lax
from jax.experimental import pallas as pl
from jax.experimental.pallas import tpu as pltpu
from jax.sharding import PartitionSpec as P

SECTIONS = 6
DIFFUSION = 0.1
CHEM_STEP = 0.02
HALO = 4
CHUNK = 4
MESH = pl.DeviceIdType.MESH
F32 = jnp.float32
BF16 = jnp.bfloat16


MIDDLE = 1.05
REACH = 0.95
TOP_CODE = 32760.0


def to_codes(scaled):
    return jnp.round(scaled).astype(jnp.int32).astype(jnp.int16)


def from_codes(codes):
    return codes.astype(jnp.int32).astype(F32)


def minmod(first, second):
    return jnp.maximum(0.0, jnp.minimum(first, second)) + jnp.minimum(
        0.0, jnp.maximum(first, second)
    )


def coefficients(a):
    size = jnp.abs(a)
    return jnp.minimum(a, 0.0) - DIFFUSION, 0.5 * size * (1.0 - size), a >= 0.0


def sweep_rows(ext, wind):
    m = ext.shape[0] - 4
    a = 0.5 * (wind[1 : m + 2] + wind[2 : m + 3])
    jump_gain, slope_gain, forward = coefficients(a)
    jumps = ext[1:] - ext[:-1]
    slopes = minmod(jumps[:-1], jumps[1:])
    flux = (
        a * ext[1 : m + 2]
        + jump_gain * jumps[1 : m + 2]
        + slope_gain * jnp.where(forward, slopes[: m + 1], slopes[1:])
    )
    return ext[2 : m + 2] - (flux[1:] - flux[:-1])


def sweep_columns(q, wind):
    columns = q.shape[2]
    last = lax.broadcasted_iota(jnp.int32, wind.shape, 2) == columns - 1
    a = jnp.where(last, 0.0, 0.5 * (wind + pltpu.roll(wind, columns - 1, 2)))
    jump_gain, slope_gain, forward = coefficients(a)
    edge = lax.broadcasted_iota(jnp.int32, q.shape, 2) == columns - 1
    jumps = jnp.where(edge, 0.0, pltpu.roll(q, columns - 1, 2) - q)
    slopes = minmod(pltpu.roll(jumps, 1, 2), jumps)
    upwind = jnp.where(forward, slopes, pltpu.roll(slopes, columns - 1, 2))
    flux = a * q + jump_gain * jumps + slope_gain * upwind
    return q - (flux - pltpu.roll(flux, 1, 2))


def kernel(
    conc_in, wind_in, k_in, react_in, prod_in, out_ref,
    conc_ref, k_ref, react_ref, prod_ref,
    ext, mid, rims_out, rims_in, codes, tops, winds, windf, codes_in, tops_in, cells, cells_left, picks, net, gain, rates, rates_left,
    wind_send, wind_recv, rim_send, halo_send, halo_recv, row_send, row_recv, load_sem,
):
    wide = lax.axis_size("wide")
    narrow = lax.axis_size("narrow")
    me = lax.axis_index("wide")
    slab = lax.axis_index("narrow")
    groups, rows, columns = conc_ref.shape
    species = cells.shape[0]
    reactions = react_ref.shape[1]
    lanes = k_ref.shape[1]
    above = lax.rem(slab + 1, narrow)
    below = lax.rem(slab + narrow - 1, narrow)

    barrier = pltpu.get_barrier_semaphore()
    for step in range(1, wide):
        pl.semaphore_signal(
            barrier, inc=1, device_id={"wide": lax.rem(me + step, wide)}, device_id_type=MESH
        )
    for other in (above, below):
        pl.semaphore_signal(barrier, inc=1, device_id={"narrow": other}, device_id_type=MESH)

    for place in range(HALO):
        pl.semaphore_signal(
            barrier, inc=1, device_id={"narrow": above, "wide": place}, device_id_type=MESH
        )
        pl.semaphore_signal(
            barrier,
            inc=1,
            device_id={"narrow": below, "wide": wide - 1 - place},
            device_id_type=MESH,
        )

    loads = [
        pltpu.make_async_copy(source, target, load_sem.at[index])
        for index, (source, target) in enumerate(
            (
                (conc_in, conc_ref),
                (react_in, react_ref),
                (prod_in, prod_ref),
                (k_in, k_ref),
                (wind_in, winds.at[HALO + me]),
            )
        )
    ]
    for copy in loads[::-1]:
        copy.start()

    low_rim = (wide - 1 - me + HALO) // wide
    high_rim = (me + HALO) // wide
    pl.semaphore_wait(barrier, wide + 1 + wide * (low_rim + high_rim))

    def wind_copy(slot, send, **device):
        return pltpu.make_async_remote_copy(
            src_ref=winds.at[HALO + me],
            dst_ref=winds.at[slot],
            send_sem=send,
            recv_sem=wind_recv.at[slot],
            device_id=device,
            device_id_type=MESH,
        )

    wind_copies = [
        wind_copy(HALO + me, wind_send.at[step], wide=lax.rem(me + step, wide))
        for step in range(1, wide)
    ]

    def rim_copies(act):
        @pl.when(me < HALO)
        def _():
            for step in range(wide):
                act(
                    wind_copy(
                        HALO + rows + me,
                        rim_send.at[0, step],
                        narrow=below,
                        wide=lax.rem(me + step, wide),
                    )
                )

        @pl.when(me >= wide - HALO)
        def _():
            for step in range(wide):
                act(
                    wind_copy(
                        me - (wide - HALO),
                        rim_send.at[1, step],
                        narrow=above,
                        wide=lax.rem(me + step, wide),
                    )
                )

    halos = [
        pltpu.make_async_remote_copy(
            src_ref=rims_out.at[side],
            dst_ref=rims_in.at[side],
            send_sem=halo_send.at[side],
            recv_sem=halo_recv.at[side],
            device_id={"narrow": other},
            device_id_type=MESH,
        )
        for side, other in enumerate((above, below))
    ]

    loads[-1].wait()
    for copy in wind_copies:
        copy.start()
    rim_copies(lambda copy: copy.start())

    loads[0].wait()
    turned = jnp.swapaxes(conc_ref[...], 0, 1)
    ext[HALO : HALO + rows] = turned
    for side, rim in enumerate((turned[rows - HALO :], turned[:HALO])):
        rims_out[side] = to_codes((rim - MIDDLE) * (TOP_CODE / REACH))
    for copy in halos:
        copy.start()

    for copy in loads[1:-1]:
        copy.wait()
    ids = lax.broadcasted_iota(jnp.int32, (species, reactions), 0)

    def one_hot(ref, which):
        return jnp.where(ids == ref[which : which + 1, :], 1.0, 0.0)

    first, second = one_hot(react_ref, 0), one_hot(react_ref, 1)
    net[...] = (one_hot(prod_ref, 0) + one_hot(prod_ref, 1) - first - second).astype(BF16)
    for index, table in enumerate((first, second)):
        picks[index] = jnp.transpose(table).astype(BF16)
    for part in range(reactions // lanes):
        constants = CHEM_STEP * k_ref[part : part + 1, :]
        gain[part * lanes : (part + 1) * lanes] = jnp.transpose(
            jnp.broadcast_to(constants, (columns, lanes))
        )
    cells_left[...] = jnp.zeros_like(cells_left)
    rates_left[...] = jnp.zeros_like(rates_left)

    def wind_arrival(slot):
        wind_copy(slot, wind_send.at[0], wide=lax.rem(me + 1, wide)).wait_recv()

    for step in range(1, wide):
        wind_arrival(HALO + lax.rem(me + step, wide))

    windf[HALO : HALO + rows] = winds[HALO : HALO + rows].astype(F32)

    def wind_of(substep, direction, start, count):
        return windf[start : start + count, substep, direction : direction + 1, :]

    def first_substep(o):
        swept = sweep_rows(ext[o : o + CHUNK + 4], wind_of(0, 0, o, CHUNK + 4))
        mid[o : o + CHUNK] = sweep_columns(swept, wind_of(0, 1, o + 2, CHUNK))

    def second_substep(g):
        swept = sweep_rows(mid[g : g + CHUNK + 4], wind_of(1, 0, g + 2, CHUNK + 4))
        value = sweep_columns(swept, wind_of(1, 1, g + 4, CHUNK))
        top = jnp.maximum(jnp.max(jnp.abs(value), axis=1, keepdims=True), 1e-30)
        codes[g : g + CHUNK] = to_codes(value * (TOP_CODE / top))
        tops[g : g + CHUNK] = top * (1.0 / TOP_CODE)

    def row_copies(row, source):
        return [
            pltpu.make_async_remote_copy(
                src_ref=here.at[row],
                dst_ref=there.at[source],
                send_sem=row_send.at[index, row],
                recv_sem=row_recv.at[index, source],
                device_id={"wide": row},
                device_id_type=MESH,
            )
            for index, (here, there) in enumerate(((codes, codes_in), (tops, tops_in)))
        ]

    others = [lax.rem(me + step, wide) for step in range(1, wide)]

    for o in range(HALO, rows, CHUNK):
        first_substep(o)
    for g in range(HALO, rows - HALO, CHUNK):
        second_substep(g)

    for slot in range(HALO):
        wind_arrival(slot)
        wind_arrival(HALO + rows + slot)
    for copy in halos:
        copy.wait_recv()
    for side, start in enumerate((0, HALO + rows)):
        ext[start : start + HALO] = from_codes(rims_in[side]) * (REACH / TOP_CODE) + MIDDLE
    windf[0:HALO] = winds[0:HALO].astype(F32)
    windf[HALO + rows :] = winds[HALO + rows :].astype(F32)
    for o in (0, rows):
        first_substep(o)
    for g in (0, rows - HALO):
        second_substep(g)
    for other in others:
        for copy in row_copies(other, me)[::-1]:
            copy.start()
    codes_in[me] = codes[me]
    tops_in[me] = tops[me]
    for other in others:
        for copy in row_copies(other, other):
            copy.wait_recv()

    for source in range(wide):
        cells[source * groups : (source + 1) * groups] = (
            from_codes(codes_in[source]) * tops_in[source]
        )

    block = species

    def section(_, carry):
        q = cells[...]
        wanted = q + cells_left[...]
        high = wanted.astype(BF16)
        cells_left[...] = wanted - high.astype(F32)
        for start in range(0, reactions, block):
            span = pl.ds(start, block)
            one = jnp.dot(picks[0, span, :], high, preferred_element_type=F32)
            two = jnp.dot(picks[1, span, :], high, preferred_element_type=F32)
            rate = gain[span, :] * one * two + rates_left[span, :]
            rounded = rate.astype(BF16)
            rates_left[span, :] = rate - rounded.astype(F32)
            rates[span, :] = rounded
        cells[...] = q + jnp.dot(net[...], rates[...], preferred_element_type=F32)
        return carry

    lax.fori_loop(0, SECTIONS, section, 0, unroll=True)
    parts = columns // lanes
    for part in range(parts):
        out_ref[pl.ds(part, species, stride=parts), :] = cells[:, part * lanes : (part + 1) * lanes]

    for copy in wind_copies:
        copy.wait_send()
    rim_copies(lambda copy: copy.wait_send())
    for copy in halos:
        copy.wait_send()
    for other in others:
        for copy in row_copies(other, me):
            copy.wait_send()


def place_kernel(result_ref, out_ref, sem):
    copy = pltpu.make_async_copy(result_ref, out_ref, sem)
    copy.start()
    copy.wait()


def on_device(wide, concentrations, wind_speeds, rate_constants, reactants, products):
    groups, rows, columns = concentrations.shape
    assert wind_speeds.shape[2] == 1 and 2 * HALO <= rows and rows == wide and rows % CHUNK == 0
    species = groups * wide
    reactions = rate_constants.shape[0]
    wind = jnp.swapaxes(wind_speeds, 1, 2).reshape(2, 2, columns)
    lanes = 128
    dma = pltpu.SemaphoreType.DMA
    inputs = (
        concentrations,
        wind,
        rate_constants.reshape(-1, lanes),
        reactants.T,
        products.T,
    )
    result = pl.pallas_call(
        kernel,
        out_shape=jax.ShapeDtypeStruct((species * columns // lanes, lanes), F32),
        in_specs=[pl.BlockSpec(memory_space=pltpu.HBM)] * 5,
        out_specs=pl.BlockSpec(memory_space=pltpu.VMEM),
        scratch_shapes=[
            pltpu.VMEM((groups, rows, columns), F32),
            pltpu.VMEM((reactions // lanes, lanes), F32),
            pltpu.VMEM((2, reactions), jnp.int32),
            pltpu.VMEM((2, reactions), jnp.int32),
            pltpu.VMEM((rows + 2 * HALO, groups, columns), F32),
            pltpu.VMEM((rows + HALO, groups, columns), F32),
            pltpu.VMEM((2, HALO, groups, columns), jnp.int16),
            pltpu.VMEM((2, HALO, groups, columns), jnp.int16),
            pltpu.VMEM((rows, groups, columns), jnp.int16),
            pltpu.VMEM((rows, 1, columns), F32),
            pltpu.VMEM((rows + 2 * HALO, 2, 2, columns), BF16),
            pltpu.VMEM((rows + 2 * HALO, 2, 2, columns), F32),
            pltpu.VMEM((wide, groups, columns), jnp.int16),
            pltpu.VMEM((wide, 1, columns), F32),
            pltpu.VMEM((species, columns), F32),
            pltpu.VMEM((species, columns), F32),
            pltpu.VMEM((2, reactions, species), BF16),
            pltpu.VMEM((species, reactions), BF16),
            pltpu.VMEM((reactions, columns), F32),
            pltpu.VMEM((reactions, columns), BF16),
            pltpu.VMEM((reactions, columns), F32),
            dma((wide,)), dma((rows + 2 * HALO,)), dma((2, wide)),
            dma((2,)), dma((2,)), dma((2, rows)), dma((2, wide)), dma((5,)),
        ],
        compiler_params=pltpu.CompilerParams(
            collective_id=0, has_side_effects=True, vmem_limit_bytes=24 * 2**20
        ),
        name="transport_chemistry",
    )(*[pltpu.with_memory_space_constraint(each, pltpu.HBM) for each in inputs])
    result = pl.pallas_call(
        place_kernel,
        out_shape=jax.ShapeDtypeStruct(result.shape, F32),
        in_specs=[pl.BlockSpec(memory_space=pltpu.VMEM)],
        out_specs=pl.BlockSpec(memory_space=pl.ANY),
        scratch_shapes=[dma(())],
        compiler_params=pltpu.CompilerParams(vmem_limit_bytes=2**20),
        name="place",
    )(result)
    return result.reshape(species, 1, columns)


def solution(mesh):
    return jax.shard_map(
        functools.partial(on_device, mesh.shape["wide"]),
        mesh=mesh,
        in_specs=(
            P("wide", "narrow", None),
            P(None, None, ("narrow", "wide"), None),
            P(),
            P(),
            P(),
        ),
        out_specs=P(None, ("narrow", "wide"), None),
        check_vma=False,
    )
```
